32 devices in a mesh: front: 8 (over y, x, core), panel: 4 (over z).
Axes of the slice: x: 2, y: 2, z: 4, core: 2. Of those that a mesh axis runs over, the one named last changes fastest.
Arguments:
- elem_tiles: bfloat16 [8, 4, 56, 128, 128], P('front', 'panel'), may hold values from -6 to 6
- targets: int32 [8, 4, 56, 1], P('front', 'panel'), may hold values from 0 to 7; in each aligned block of 56 rows (0 to 55, 56 to 111, ..., all dimensions but the last counted through in order) at most 14 rows name the same one
- tile_places: int32 [8, 4, 56], P('front', 'panel'), may hold values from 0 to 63, as said below
- friction: float32 [8, 2048], P('front'), may hold values from 0.25 to 4
Outputs:
- parent_half: float32 [8, 1536, 768], P('front', 'panel')
The draws below stay inside these ranges and needn't reach their ends.
Inputs may be any that keep to these rules, and one draw needn't show every extreme that they name: `targets`: in the 56 tiles of one device at most 14 have the same target, and some target has exactly 14. `tile_places`: A place j * 16 + c of a tile on panel index p has j < 4 and c <= j * 4 + p, so tiles lie on or below the diagonal.
All inputs are finite; a program needn't handle non-finite values.
Results may differ from the reference program's by a relative error of at most 0.0003.
Values may be sent and summed in bfloat16 or wider, within the bound.
A program may use at most 128 MiB of HBM per device.

```python
import math
import jax
import jax.numpy as jnp
import numpy as np
from jax import lax

F = 2048
TILE = 128
P_SIZE = 512
NB_DEV = 56
CAP = 14
ROWT = 4
NCT = 16
SCH = 1536
HALF = 768
N_FRONT = 8
N_PANEL = 4


def draw_tile_places(key, part):
    key_row, key_col = jax.random.split(jax.random.fold_in(key, 7))
    shape = (N_FRONT, N_PANEL, NB_DEV)
    row_tile = jax.random.randint(key_row, shape, 0, ROWT, dtype=jnp.int32)
    row_tile = row_tile.at[:, :, 0].set(ROWT - 1)
    row_tile = row_tile.at[:, :, 1].set(0)
    panel_pos = jnp.arange(N_PANEL, dtype=jnp.int32)[None, :, None]
    limit = row_tile * N_PANEL + panel_pos + 1
    column = jax.random.randint(key_col, shape, 0, limit, dtype=jnp.int32)
    column = column.at[:, :, 0].set(limit[:, :, 0] - 1)
    column = column.at[:, :, 1].set(0)
    return row_tile * NCT + column


def shard_levels(key, extent, cuts, low, largest):
    def one(dim, shards_of):
        draws = jax.random.uniform(jax.random.fold_in(jax.random.fold_in(key, 6), dim), (shards_of,), jnp.float32, low / len(cuts), largest / len(cuts))
        return jnp.repeat(jnp.exp(draws), extent[dim] // shards_of).reshape((-1,) + (1,) * (len(extent) - dim - 1))

    loudness = one(*cuts[0])
    for cut in cuts[1:]:
        loudness = loudness * one(*cut)
    return loudness


def assign_block(rng, own, number, rows, number_of, top, most, lean):
    order = jax.random.permutation(rng, number_of)
    packed, usual = shares(number_of, rows * top, most, lean, True), shares(number_of, rows * top, most, lean, False)
    places = jnp.arange(number_of)

    def named(sizes, rotation):
        used = int((sizes > 0).sum())
        fixed = max(1, used // 4)
        shifted = fixed + (places - fixed + rotation * (used - fixed)) % max(1, number_of - fixed)
        return jnp.zeros((number_of,), jnp.int32).at[order[jnp.where(places < fixed, places, shifted)]].set(jnp.asarray(sizes, jnp.int32))

    sizes = jnp.where(number % 4 == 0, named(packed, number // 4), named(usual, number - number // 4 - 1))
    mixed = jax.random.permutation(jax.random.fold_in(own, 3), number_of)
    donor, sink = mixed[0:number_of // 2 * 2:2], mixed[1:number_of // 2 * 2:2]
    room = jnp.minimum(sizes[donor] - 1, most - sizes[sink]) // 2
    room = jnp.where((donor == order[0]) | (sink == order[0]) | (sizes[sink] == 0), 0, jnp.maximum(room, 0))
    shifted = jax.random.randint(jax.random.fold_in(own, 4), (number_of // 2,), 0, 1 << 20) % (room + 1)
    sizes = sizes.at[donor].add(-shifted).at[sink].add(shifted)
    members = jnp.searchsorted(jnp.cumsum(sizes), jnp.arange(rows * top), side="right").astype(jnp.int32)
    grid = members.reshape(top, rows).T
    grid = grid[jax.random.permutation(jax.random.fold_in(own, 1), rows)]
    rotation = jax.random.randint(jax.random.fold_in(own, 2), (rows, 1), 0, top)
    return jnp.take_along_axis(grid, (jnp.arange(top)[None, :] + rotation) % top, axis=1)


def shares(count, total, most, slope, full):
    loads = [(1 << 20) // math.isqrt(standing ** slope) + 1 for standing in range(1, count + 1)]
    largest = most if full else min(most, max(-(-total // count), total * loads[0] // sum(loads)))
    least = 1 if total - largest >= count - 1 else 0
    given, surplus = [largest] + [least] * (count - 1), total - largest - least * (count - 1)
    while surplus > 0:
        movable = [i for i in range(1, count) if given[i] < largest] or [i for i in range(1, count) if given[i] < most]
        pool, left = sum([loads[i] for i in movable]), surplus
        for i in movable:
            extra = min(most - given[i], max(1, left * loads[i] // pool), surplus)
            given[i] = given[i] + extra
            surplus = surplus - extra
    return np.array(given)


def gaussian(own_key, shape, deviation, most, pieces=(), held_as=jnp.bfloat16):
    entries = jax.random.normal(own_key, shape, jnp.float32) * deviation
    if len(pieces) > 0:
        entries = shard_levels(own_key, shape, pieces, -0.22, 0.18) * entries
    return jnp.clip(entries, min=-most, max=most).astype(held_as)


def setup_inputs(seed: int = 0) -> dict:
    key_of = jax.random.split(jax.random.key(seed), 5)
    elem_tiles = gaussian(key_of[0], (N_FRONT, N_PANEL, NB_DEV, TILE, TILE), 1.0, 6.0, ((0, 8), (1, 4)))
    targets_keys = jax.random.split(jax.random.fold_in(key_of[1], 1), N_FRONT * N_PANEL * NB_DEV // NB_DEV)
    targets_turns = jax.random.permutation(jax.random.fold_in(key_of[1], 3), N_FRONT * N_PANEL * NB_DEV // NB_DEV)
    targets = jax.vmap(lambda own, number: assign_block(jax.random.fold_in(key_of[1], 2), own, number, NB_DEV, N_FRONT, 1, CAP, 2))(targets_keys, targets_turns).reshape((N_FRONT, N_PANEL, NB_DEV, 1))
    tile_places = draw_tile_places(jax.random.fold_in(key_of[4], 71), 0)
    friction = jnp.clip(jnp.exp(math.log(4.0) - 2.7725887 * jax.random.uniform(key_of[3], (N_FRONT, F), jnp.float32) ** shard_levels(key_of[3], (N_FRONT, F), ((0, 8),), -0.2, 0.2)), 0.25, 4.0)
    return dict(elem_tiles=elem_tiles, targets=targets, tile_places=tile_places, friction=friction)


def front_update(matrix, fric):
    lower = jnp.tril(matrix, -1)
    lower_b = lower.astype(jnp.bfloat16)
    gram = jnp.dot(lower_b.astype(jnp.float32), lower_b.T.astype(jnp.float32), preferred_element_type=jnp.float32) / F
    full = gram + jnp.diag(fric)
    factor = jnp.linalg.cholesky(full[:P_SIZE, :P_SIZE])
    below = jax.scipy.linalg.solve_triangular(factor, full[P_SIZE:, :P_SIZE].T, lower=True).T
    schur = full[P_SIZE:, P_SIZE:] - jnp.dot(below, below.T, precision=lax.Precision.HIGHEST)
    schur = jnp.tril(schur)
    shaped = schur.reshape(ROWT - 1, N_PANEL, TILE, ROWT - 1, N_PANEL, TILE)
    return shaped.transpose(1, 0, 2, 4, 3, 5).reshape(SCH, SCH)

def reference(elem_tiles, targets, tile_places, friction):
    groups = N_FRONT
    panels = N_PANEL
    count = NB_DEV
    positions = ROWT * NCT
    target = targets[..., 0]
    hits = (target[..., None] == jnp.arange(groups, dtype=jnp.int32)).astype(jnp.int32)
    rank = jnp.sum((jnp.cumsum(hits, axis=2) - hits) * hits, axis=3).astype(jnp.int32)
    src_grid = jnp.broadcast_to(jnp.arange(groups, dtype=jnp.int32)[:, None, None], target.shape)
    pan_grid = jnp.broadcast_to(jnp.arange(panels, dtype=jnp.int32)[None, :, None], target.shape)
    num_grid = jnp.broadcast_to(jnp.arange(count, dtype=jnp.int32)[None, None, :], target.shape)
    index_table = jnp.zeros((groups, panels, groups, CAP), jnp.int32)
    index_table = index_table.at[target, pan_grid, src_grid, rank].set(num_grid)
    place_table = jnp.zeros((groups, panels, groups, CAP), jnp.int32)
    place_table = place_table.at[target, pan_grid, src_grid, rank].set(tile_places + 1)
    src_small = jnp.broadcast_to(jnp.arange(groups, dtype=jnp.int32)[None, :, None], (panels, groups, CAP))
    pan_small = jnp.broadcast_to(jnp.arange(panels, dtype=jnp.int32)[:, None, None], (panels, groups, CAP))

    def one_front(front_id):
        chosen = index_table[front_id]
        placed = place_table[front_id]
        picked = elem_tiles[src_small, pan_small, chosen].astype(jnp.float32)
        segment = jnp.where(placed > 0, pan_small * positions + placed - 1, panels * positions)
        blocks = jax.ops.segment_sum(picked.reshape(-1, TILE, TILE), segment.reshape(-1), num_segments=panels * positions + 1)[:-1]
        shaped = blocks.reshape(panels, ROWT, NCT, TILE, TILE).transpose(1, 0, 3, 2, 4)
        return front_update(shaped.reshape(F, F), friction[front_id])

    def one_pair(pair_id):
        summed = one_front(2 * pair_id) + one_front(2 * pair_id + 1)
        return jnp.stack([summed[:, :HALF], summed[:, HALF:]])
    result = lax.map(one_pair, jnp.arange(groups // 2, dtype=jnp.int32))
    return result.reshape(groups, SCH, HALF)
```

```python
import functools

import jax
import jax.numpy as jnp
from jax import lax
from jax.experimental import pallas as pl
from jax.experimental.pallas import tpu as pltpu
from jax.sharding import PartitionSpec as P

F32 = jnp.float32
BF16 = jnp.bfloat16
HEADER = 16
NN = (((1,), (0,)), ((), ()))
NT = (((1,), (1,)), ((), ()))
VMEM = pl.BlockSpec(memory_space=pltpu.VMEM)
SMEM = pl.BlockSpec(memory_space=pltpu.SMEM)


def split(x):
    hi = x.astype(BF16)
    return hi, (x - hi.astype(F32)).astype(BF16)


def dot(a, b, dims):
    return lax.dot_general(a, b, dims, preferred_element_type=F32)


def dot3(a, b, dims):
    ah, al = split(a)
    bh, bl = split(b)
    return dot(ah, bh, dims) + (dot(ah, bl, dims) + dot(al, bh, dims))


def pack_kernel(slots, target_ref, place_ref, tiles_ref, out_ref, count_ref, header_ref):
    tiles, edge = tiles_ref.shape[0], tiles_ref.shape[1]
    groups = out_ref.shape[0]
    header_ref[...] = jnp.zeros_like(header_ref)

    def clear(g, carry):
        count_ref[g] = 0
        return carry

    lax.fori_loop(0, groups, clear, 0)
    lane = lax.broadcasted_iota(jnp.int32, (1, edge), 1)

    def one(i, carry):
        t = target_ref[i]
        r = count_ref[t]
        count_ref[t] = r + 1
        out_ref[t, pl.ds(pl.multiple_of(r * edge, edge), edge), :] = tiles_ref[i]
        mark = (place_ref[i] + 1).astype(F32)
        header_ref[t] = jnp.where(lane == r, mark, header_ref[t])
        return carry

    lax.fori_loop(0, tiles, one, 0)

    def finish(g, carry):
        out_ref[g, pl.ds(slots * edge, HEADER), :] = jnp.broadcast_to(
            header_ref[g], (HEADER, edge)
        ).astype(BF16)
        return carry

    lax.fori_loop(0, groups, finish, 0)


def assemble_kernel(slots, panels, local_tiles, col_tiles, ids_ref, place_ref, arrived_ref, head_ref, below_ref, acc_ref):
    groups = arrived_ref.shape[0]
    edge = arrived_ref.shape[2]
    me = ids_ref[0]

    def clear(i, carry):
        acc_ref[i] = jnp.zeros((edge, edge), F32)
        return carry

    lax.fori_loop(0, local_tiles * col_tiles, clear, 0)

    def one_group(g, carry):
        def one(s, carry):
            place = place_ref[g, s]

            @pl.when(place > 0)
            def _():
                tile = arrived_ref[g, pl.ds(pl.multiple_of(s * edge, edge), edge), :]
                acc_ref[place - 1] += tile.astype(F32)

            return carry

        return lax.fori_loop(0, slots, one, carry)

    lax.fori_loop(0, groups, one_group, 0)
    row = lax.broadcasted_iota(jnp.int32, (edge, edge), 0)
    col = lax.broadcasted_iota(jnp.int32, (edge, edge), 1)
    start = 0
    for j in range(local_tiles):
        for c in range((j + 1) * panels):
            tile = acc_ref[j * col_tiles + c]
            if c >= j * panels:
                tile = jnp.where(c * edge + col < (j * panels + me) * edge + row, tile, 0.0)
            tile = tile.astype(BF16)
            if j == 0:
                head_ref[:, c * edge : (c + 1) * edge] = tile
            else:
                below_ref[:, start + c * edge : start + (c + 1) * edge] = tile
        if j > 0:
            start += (j + 1) * panels * edge


def invert_unit(block):
    edge = block.shape[0]
    count = edge // 8
    sub = lax.broadcasted_iota(jnp.int32, (8, edge), 0)
    lane = lax.broadcasted_iota(jnp.int32, (8, edge), 1)
    a = [block[8 * g : 8 * g + 8] for g in range(count)]
    e = [jnp.where(lane == sub + 8 * g, 1.0, 0.0).astype(F32) for g in range(count)]
    inv = [None] * count
    for k in range(edge):
        g, s = divmod(k, 8)
        a_row = a[g][s : s + 1]
        e_row = e[g][s : s + 1]
        pivot = jnp.broadcast_to(a_row[:, k : k + 1], (8, edge))
        flip = 1.0 / pivot
        inv[g] = flip if s == 0 else jnp.where(sub >= s, flip, inv[g])
        qa = jnp.broadcast_to(a_row, (8, edge)) * flip
        qe = jnp.broadcast_to(e_row, (8, edge)) * flip
        for i in range(g, count):
            if i == g and s == 7:
                continue
            column = jnp.broadcast_to(a[i][:, k : k + 1], (8, edge))
            if i == g:
                column = jnp.where(sub > s, column, 0.0)
            a[i] = a[i] - column * qa
            e[i] = e[i] - column * qe
    return jnp.concatenate(e, axis=0), jnp.concatenate(inv, axis=0)


def factor_kernel(width, head_ref, fric_ref, below_ref, high_ref, low_ref, a_ref, e_ref, d_ref):
    edge = below_ref.shape[0]
    order = head_ref.shape[0]
    blocks = order // edge
    head = head_ref[...]
    gram = dot(head, head, NT) * (1.0 / width)
    row = lax.broadcasted_iota(jnp.int32, (order, order), 0)
    col = lax.broadcasted_iota(jnp.int32, (order, order), 1)
    eye = row == col
    a_ref[...] = gram + jnp.where(eye, fric_ref[...], 0.0)
    e_ref[...] = jnp.where(eye, 1.0, 0.0).astype(F32)
    below_rows = lax.broadcasted_iota(jnp.int32, (order, 1), 0)

    def stage(b, carry):
        here = pl.ds(pl.multiple_of(b * edge, edge), edge)
        unit, flip = invert_unit(a_ref[here, here])
        up = dot3(unit, a_ref[here, :], NN)
        ue = dot3(unit, e_ref[here, :], NN)
        left = dot3(a_ref[:, here], unit, NT)
        left = jnp.where(below_rows >= (b + 1) * edge, left, 0.0)
        scale = jnp.concatenate([flip] * blocks, axis=1)
        e_ref[here, :] = ue
        d_ref[here, :] = scale
        a_ref[...] -= dot3(left, up * scale, NN)
        e_ref[...] -= dot3(left, ue * scale, NN)
        return carry

    lax.fori_loop(0, blocks, stage, 0)
    eh, el = split(e_ref[...])
    guess = dot(eh, head, NN) + dot(el, head, NN)
    gh, gl = split(guess)
    dh, dl = split(guess * (d_ref[...] * (1.0 / width)))
    start = 0
    for j in range(high_ref.shape[0] // edge):
        mine = below_ref[:, start : start + order]
        start += (j + 2) * order
        vh, vl = split(dot(mine, gh, NT) + dot(mine, gl, NT))
        done = mine.astype(F32) - (dot(vh, dh, NN) + (dot(vh, dl, NN) + dot(vl, dh, NN)))
        th, tl = split(done)
        high_ref[j * edge : (j + 1) * edge, :] = th
        low_ref[j * edge : (j + 1) * edge, :] = tl


def schur_kernel(width, panels, flip_side, ids_ref, high_ref, low_ref, below_ref, fric_ref, all_ref, out_ref):
    edge = below_ref.shape[0]
    order = high_ref.shape[1]
    rows = high_ref.shape[0] // edge
    half = panels // 2
    me = ids_ref[0]
    side = ids_ref[1]
    part = 1 - side if flip_side else side
    picked = pl.ds(pl.multiple_of(part * half * edge, edge), half * edge)
    starts = [0]
    for j in range(rows):
        starts.append(starts[-1] + (j + 2) * order)
    row = lax.broadcasted_iota(jnp.int32, (edge, edge), 0)
    col = lax.broadcasted_iota(jnp.int32, (edge, edge), 1)
    for jc in range(rows):
        first = starts[jc]
        last = first + (jc + 2) * order
        span = (jc + 1) * order
        theirs = all_ref[picked, first : first + order]
        rest = all_ref[picked, first + order : last]
        mine = jnp.concatenate(
            [below_ref[:, starts[j] + order : starts[j] + order + span] for j in range(jc, rows)], axis=0
        )
        total = dot(mine, rest, NT)
        total += dot(high_ref[jc * edge :, :], theirs, NT)
        total += dot(low_ref[jc * edge :, :], theirs, NT)
        total = total * (1.0 / width)
        for q in range(half):
            owner = part * half + q
            cols = slice(q * rows * edge + jc * edge, q * rows * edge + (jc + 1) * edge)
            for j in range(rows):
                if j < jc:
                    out_ref[j * edge : (j + 1) * edge, cols] = jnp.zeros((edge, edge), F32)
                    continue
                tile = total[(j - jc) * edge : (j - jc + 1) * edge, q * edge : (q + 1) * edge]
                if j == jc:
                    fric = fric_ref[(j + 1) * panels + me]
                    tile += jnp.where((row == col) & (owner == me), fric, 0.0)
                    tile = jnp.where(owner * edge + col <= me * edge + row, tile, 0.0)
                out_ref[j * edge : (j + 1) * edge, cols] = tile


def per_device(elem_tiles, targets, tile_places, friction):
    groups = lax.axis_size("front")
    panels = lax.axis_size("panel")
    count = elem_tiles.shape[2]
    edge = elem_tiles.shape[3]
    width = friction.shape[1]
    col_tiles = width // edge
    local_tiles = col_tiles // panels
    order = edge * panels
    slots = max(2, (2 * count + groups - 1) // groups)
    ids = jnp.stack([lax.axis_index("panel"), lax.axis_index("front") % 2]).astype(jnp.int32)

    packed = pl.pallas_call(
        functools.partial(pack_kernel, slots),
        out_shape=jax.ShapeDtypeStruct((groups, slots * edge + HEADER, edge), BF16),
        in_specs=[SMEM, SMEM, VMEM],
        out_specs=VMEM,
        scratch_shapes=[pltpu.SMEM((groups,), jnp.int32), pltpu.VMEM((groups, 1, edge), F32)],
        name="pack",
    )(targets.reshape(count), tile_places.reshape(count), elem_tiles.reshape(count, edge, edge))
    arrived = lax.all_to_all(packed, "front", split_axis=0, concat_axis=0, tiled=True)
    places = arrived[:, slots * edge, :slots].astype(jnp.int32)
    spread = sum((j + 1) * order for j in range(1, local_tiles))
    head, below = pl.pallas_call(
        functools.partial(assemble_kernel, slots, panels, local_tiles, col_tiles),
        out_shape=(
            jax.ShapeDtypeStruct((edge, order), BF16),
            jax.ShapeDtypeStruct((edge, spread), BF16),
        ),
        in_specs=[SMEM, SMEM, VMEM],
        out_specs=(VMEM, VMEM),
        scratch_shapes=[pltpu.VMEM((local_tiles * col_tiles, edge, edge), F32)],
        name="assemble",
    )(ids, places, arrived)
    head_rows = lax.all_gather(head, "panel", axis=0, tiled=True)
    all_rows = lax.all_gather(below, "panel", axis=0, tiled=True)
    rows = (local_tiles - 1) * edge
    high, low = pl.pallas_call(
        functools.partial(factor_kernel, width),
        out_shape=(
            jax.ShapeDtypeStruct((rows, order), BF16),
            jax.ShapeDtypeStruct((rows, order), BF16),
        ),
        in_specs=[VMEM, VMEM, VMEM],
        out_specs=(VMEM, VMEM),
        scratch_shapes=[pltpu.VMEM((order, order), F32)] * 3,
        cost_estimate=pl.CostEstimate(flops=30_000_000_000, bytes_accessed=4_000_000, transcendentals=0),
        name="factor",
    )(head_rows, friction[:, :order], below)

    def schur_half(flip_side):
        return pl.pallas_call(
            functools.partial(schur_kernel, width, panels, flip_side),
            out_shape=jax.ShapeDtypeStruct((rows, rows * panels // 2), F32),
            in_specs=[SMEM, VMEM, VMEM, VMEM, VMEM, VMEM],
            out_specs=VMEM,
            cost_estimate=pl.CostEstimate(flops=1_000_000_000, bytes_accessed=4_000_000, transcendentals=0),
            name="schur_other" if flip_side else "schur_keep",
        )(ids, high, low, below, friction.reshape(col_tiles, 1, edge), all_rows)

    other = schur_half(True)
    partner = lax.ppermute(other, "front", [(i, i ^ 1) for i in range(groups)])
    keep = schur_half(False)
    return (keep + partner)[None]


def solution(mesh):
    return jax.shard_map(
        per_device,
        mesh=mesh,
        in_specs=(
            P("front", "panel", None, None, None),
            P("front", "panel", None, None),
            P("front", "panel", None),
            P("front", None),
        ),
        out_specs=P("front", "panel", None),
        check_vma=False,
    )
```

```python
import functools

import jax
import jax.numpy as jnp
from jax import lax
from jax.experimental import pallas as pl
from jax.experimental.pallas import tpu as pltpu
from jax.sharding import PartitionSpec as P

F32 = jnp.float32
BF16 = jnp.bfloat16
HEADER = 16
NN = (((1,), (0,)), ((), ()))
NT = (((1,), (1,)), ((), ()))
VMEM = pl.BlockSpec(memory_space=pltpu.VMEM)
SMEM = pl.BlockSpec(memory_space=pltpu.SMEM)


def split(x):
    hi = x.astype(BF16)
    return hi, (x - hi.astype(F32)).astype(BF16)


def dot(a, b, dims):
    return lax.dot_general(a, b, dims, preferred_element_type=F32)


def dot3(a, b, dims):
    ah, al = split(a)
    bh, bl = split(b)
    return dot(ah, bh, dims) + (dot(ah, bl, dims) + dot(al, bh, dims))


def pack_kernel(slots, target_ref, place_ref, tiles_ref, out_ref, count_ref, header_ref):
    tiles, edge = tiles_ref.shape[0], tiles_ref.shape[1]
    groups = out_ref.shape[0]
    header_ref[...] = jnp.zeros_like(header_ref)

    def clear(g, carry):
        count_ref[g] = 0
        return carry

    lax.fori_loop(0, groups, clear, 0)
    lane = lax.broadcasted_iota(jnp.int32, (1, edge), 1)

    def one(i, carry):
        t = target_ref[i]
        r = count_ref[t]
        count_ref[t] = r + 1
        out_ref[t, pl.ds(pl.multiple_of(r * edge, edge), edge), :] = tiles_ref[i]
        mark = (place_ref[i] + 1).astype(F32)
        header_ref[t] = jnp.where(lane == r, mark, header_ref[t])
        return carry

    lax.fori_loop(0, tiles, one, 0)

    def finish(g, carry):
        out_ref[g, pl.ds(slots * edge, HEADER), :] = jnp.broadcast_to(
            header_ref[g], (HEADER, edge)
        ).astype(BF16)
        return carry

    lax.fori_loop(0, groups, finish, 0)


def assemble_kernel(slots, panels, local_tiles, col_tiles, ids_ref, place_ref, arrived_ref, head_ref, below_ref, acc_ref):
    groups = arrived_ref.shape[0]
    edge = arrived_ref.shape[2]
    me = ids_ref[0]

    def clear(i, carry):
        acc_ref[i] = jnp.zeros((edge, edge), F32)
        return carry

    lax.fori_loop(0, local_tiles * col_tiles, clear, 0)

    def one_group(g, carry):
        def one(s, carry):
            place = place_ref[g, s]

            @pl.when(place > 0)
            def _():
                tile = arrived_ref[g, pl.ds(pl.multiple_of(s * edge, edge), edge), :]
                acc_ref[place - 1] += tile.astype(F32)

            return carry

        return lax.fori_loop(0, slots, one, carry)

    lax.fori_loop(0, groups, one_group, 0)
    row = lax.broadcasted_iota(jnp.int32, (edge, edge), 0)
    col = lax.broadcasted_iota(jnp.int32, (edge, edge), 1)
    start = 0
    for j in range(local_tiles):
        for c in range((j + 1) * panels):
            tile = acc_ref[j * col_tiles + c]
            if c >= j * panels:
                tile = jnp.where(c * edge + col < (j * panels + me) * edge + row, tile, 0.0)
            tile = tile.astype(BF16)
            if j == 0:
                head_ref[:, c * edge : (c + 1) * edge] = tile
            else:
                below_ref[:, start + c * edge : start + (c + 1) * edge] = tile
        if j > 0:
            start += (j + 1) * panels * edge


def eliminate(block):
    edge = block.shape[0]
    count = edge // 8
    sub = lax.broadcasted_iota(jnp.int32, (8, edge), 0)
    lane = lax.broadcasted_iota(jnp.int32, (8, edge), 1)
    a = [block[8 * g : 8 * g + 8] for g in range(count)]
    e = [jnp.where(lane == sub + 8 * g, 1.0, 0.0).astype(F32) for g in range(count)]
    q = []

    def across(x, k):
        return jnp.broadcast_to(x[:, k : k + 1], (8, edge))

    def down(x, k):
        return jnp.broadcast_to(x[k : k + 1], (8, edge))

    for g in range(count):
        work = [across(a[g], 8 * g + s) for s in range(8)] + [a[g], e[g]]
        for s in range(0, 8, 2):
            u, v = work[s], work[s + 1]
            p11, p21, p12, p22 = down(u, s), down(u, s + 1), down(v, s), down(v, s + 1)
            flip = 1.0 / (p11 * p22 - p12 * p21)
            p11, p21, p12, p22 = p11 * flip, p21 * flip, p12 * flip, p22 * flip
            for t in range(s + 2, 10):
                x = work[t]
                x1, x2 = down(x, s), down(x, s + 1)
                y1 = p22 * x1 - p12 * x2
                y2 = p11 * x2 - p21 * x1
                x = x - u * y1 - v * y2
                work[t] = jnp.where(sub == s, y1, jnp.where(sub == s + 1, y2, x))
        qa, qe = work[8], work[9]
        q.append(qe)
        if g + 1 < count:
            ra = [down(qa, s) for s in range(8)]
            re = [down(qe, s) for s in range(8)]
        for i in range(g + 1, count):
            xa, xe = a[i], e[i]
            cols = [across(xa, 8 * g + s) for s in range(8)]
            for s in range(8):
                xa = xa - cols[s] * ra[s]
                xe = xe - cols[s] * re[s]
            a[i], e[i] = xa, xe
    return jnp.concatenate(e, axis=0), jnp.concatenate(q, axis=0)


def stages(first, last, edge, a_ref, e_ref, q_ref):
    order = a_ref.shape[0]
    below_rows = lax.broadcasted_iota(jnp.int32, (order, 1), 0)

    def stage(b, carry):
        here = pl.ds(pl.multiple_of(b * edge, edge), edge)
        unit, ready = eliminate(a_ref[here, here])
        up = dot3(ready, a_ref[here, :], NN)
        ue = dot3(ready, e_ref[here, :], NN)
        left = dot3(a_ref[:, here], unit, NT)
        left = jnp.where(below_rows >= (b + 1) * edge, left, 0.0)
        e_ref[here, :] = dot3(unit, e_ref[here, :], NN)
        q_ref[here, :] = ue
        a_ref[...] -= dot3(left, up, NN)
        e_ref[...] -= dot3(left, ue, NN)
        return carry

    lax.fori_loop(first, last, stage, 0)


def factor_start(width, edge, last, head_ref, fric_ref, a_ref, e_ref, q_ref):
    order = head_ref.shape[0]
    head = head_ref[...]
    gram = dot(head, head, NT) * (1.0 / width)
    row = lax.broadcasted_iota(jnp.int32, (order, order), 0)
    col = lax.broadcasted_iota(jnp.int32, (order, order), 1)
    eye = row == col
    a_ref[...] = gram + jnp.where(eye, fric_ref[...], 0.0)
    e_ref[...] = jnp.where(eye, 1.0, 0.0).astype(F32)
    stages(0, last, edge, a_ref, e_ref, q_ref)


def factor_end(width, edge, first, head_ref, below_ref, a_in, e_in, q_in, high_ref, low_ref, a_ref, e_ref, q_ref):
    order = head_ref.shape[0]
    a_ref[...] = a_in[...]
    e_ref[...] = e_in[...]
    q_ref[...] = q_in[...]
    stages(first, order // edge, edge, a_ref, e_ref, q_ref)
    head = head_ref[...]
    eh, el = split(e_ref[...])
    gh, gl = split(dot(eh, head, NN) + dot(el, head, NN))
    qh, ql = split(q_ref[...])
    dh, dl = split((dot(qh, head, NN) + dot(ql, head, NN)) * (1.0 / width))
    start = 0
    for j in range(high_ref.shape[0] // edge):
        mine = below_ref[:, start : start + order]
        start += (j + 2) * order
        vh, vl = split(dot(mine, gh, NT) + dot(mine, gl, NT))
        done = mine.astype(F32) - (dot(vh, dh, NN) + (dot(vh, dl, NN) + dot(vl, dh, NN)))
        th, tl = split(done)
        high_ref[j * edge : (j + 1) * edge, :] = th
        low_ref[j * edge : (j + 1) * edge, :] = tl


def trimmed(rows, panels, hops):
    return [(j + 1) * panels - hops for j in range(1, rows + 1)]


def shorten(array, old, new, edge):
    parts, start = [], 0
    for was, now in zip(old, new):
        parts.append(array[:, start * edge : (start + now) * edge])
        start += was
    return jnp.concatenate(parts, axis=1)


def owner_block(width, panels, me, side, owner, own, counts, theirs_ref, high_ref, low_ref, below_ref, fric_ref, out_ref):
    edge = below_ref.shape[0]
    order = high_ref.shape[1]
    rows = high_ref.shape[0] // edge
    half = panels // 2
    starts = [0]
    for j in range(rows):
        starts.append(starts[-1] + (j + 2) * order)
    place = (owner // half + side) % 2
    base = (owner % half) * (rows * edge)
    row = lax.broadcasted_iota(jnp.int32, (edge, edge), 0)
    col = lax.broadcasted_iota(jnp.int32, (edge, edge), 1)
    first = 0
    for jc in range(rows):
        cols = pl.ds(pl.multiple_of(base + jc * edge, edge), edge)
        if jc > 0:
            out_ref[place, : jc * edge, cols] = jnp.zeros((jc * edge, edge), F32)
        if jc >= len(counts):
            out_ref[place, jc * edge :, cols] = jnp.zeros(((rows - jc) * edge, edge), F32)
            continue
        last = first + counts[jc] * edge
        span = counts[jc] * edge - order
        mine = jnp.concatenate(
            [below_ref[:, starts[j] + order : starts[j] + order + span] for j in range(jc, rows)], axis=0
        )
        total = dot(mine, theirs_ref[:, first + order : last], NT)
        total += dot(high_ref[jc * edge :, :], theirs_ref[:, first : first + order], NT)
        total += dot(low_ref[jc * edge :, :], theirs_ref[:, first : first + order], NT)
        total = total * (1.0 / width)
        first = last
        top = total[:edge]
        if own:
            top += jnp.where(row == col, fric_ref[(jc + 1) * panels + me], 0.0)
        top = jnp.where(owner * edge + col <= me * edge + row, top, 0.0)
        out_ref[place, jc * edge : (jc + 1) * edge, cols] = top
        if jc + 1 < rows:
            out_ref[place, (jc + 1) * edge :, cols] = total[edge:]


def schur_kernel(width, panels, hops, own, aliased, ids_ref, high_ref, low_ref, below_ref, fric_ref, *rest):
    rest = list(rest)
    out_ref = rest.pop()
    if aliased:
        out_ref[...] = rest.pop()[...]
    me = ids_ref[0]
    side = ids_ref[1]
    rows = high_ref.shape[0] // below_ref.shape[0]
    run = functools.partial(owner_block, width, panels, me, side)
    shared = (high_ref, low_ref, below_ref, fric_ref, out_ref)
    if own:
        run(me, True, trimmed(rows, panels, 0), below_ref, *shared)
    for hop, up_ref, down_ref in zip(hops, rest[0::2], rest[1::2]):

        @pl.when(me >= hop)
        def _():
            run(me - hop, False, trimmed(rows, panels, hop), up_ref, *shared)

        @pl.when(me + hop < panels)
        def _():
            run(me + hop, False, trimmed(rows, panels, 0)[:-1], down_ref, *shared)


def per_device(elem_tiles, targets, tile_places, friction):
    groups = lax.axis_size("front")
    panels = lax.axis_size("panel")
    count = elem_tiles.shape[2]
    edge = elem_tiles.shape[3]
    width = friction.shape[1]
    col_tiles = width // edge
    local_tiles = col_tiles // panels
    order = edge * panels
    slots = max(2, (2 * count + groups - 1) // groups)
    ids = jnp.stack([lax.axis_index("panel"), lax.axis_index("front") % 2]).astype(jnp.int32)

    packed = pl.pallas_call(
        functools.partial(pack_kernel, slots),
        out_shape=jax.ShapeDtypeStruct((groups, slots * edge + HEADER, edge), BF16),
        in_specs=[SMEM, SMEM, VMEM],
        out_specs=VMEM,
        scratch_shapes=[pltpu.SMEM((groups,), jnp.int32), pltpu.VMEM((groups, 1, edge), F32)],
        name="pack",
    )(targets.reshape(count), tile_places.reshape(count), elem_tiles.reshape(count, edge, edge))
    arrived = lax.all_to_all(packed, "front", split_axis=0, concat_axis=0, tiled=True)
    places = arrived[:, slots * edge, :slots].astype(jnp.int32)
    spread = sum((j + 1) * order for j in range(1, local_tiles))
    head, below = pl.pallas_call(
        functools.partial(assemble_kernel, slots, panels, local_tiles, col_tiles),
        out_shape=(
            jax.ShapeDtypeStruct((edge, order), BF16),
            jax.ShapeDtypeStruct((edge, spread), BF16),
        ),
        in_specs=[SMEM, SMEM, VMEM],
        out_specs=(VMEM, VMEM),
        scratch_shapes=[pltpu.VMEM((local_tiles * col_tiles, edge, edge), F32)],
        name="assemble",
    )(ids, places, arrived)
    head_rows = lax.all_gather(head, "panel", axis=0, tiled=True)
    rows_below = local_tiles - 1
    rows = rows_below * edge
    fric_tiles = friction.reshape(col_tiles, 1, edge)
    climb = [(i, i + 1) for i in range(panels - 1)]
    sink = [(i + 1, i) for i in range(panels - 1)]
    ups, downs = [], []
    up, was = below, trimmed(rows_below, panels, 0)
    down = below[:, : sum(was[:-1]) * edge]
    for hop in range(1, panels):
        now = trimmed(rows_below, panels, hop)
        up = lax.ppermute(shorten(up, was, now, edge), "panel", climb)
        down = lax.ppermute(down, "panel", sink)
        was = now
        ups.append(up)
        downs.append(down)
    square = jax.ShapeDtypeStruct((order, order), F32)
    middle = panels // 2
    state = pl.pallas_call(
        functools.partial(factor_start, width, edge, middle),
        out_shape=(square,) * 3,
        in_specs=[VMEM, VMEM],
        out_specs=(VMEM,) * 3,
        cost_estimate=pl.CostEstimate(flops=15_000_000_000, bytes_accessed=4_000_000, transcendentals=0),
        name="factor_start",
    )(head_rows, friction[:, :order])
    high, low = pl.pallas_call(
        functools.partial(factor_end, width, edge, middle),
        out_shape=(jax.ShapeDtypeStruct((rows, order), BF16),) * 2,
        in_specs=[VMEM] * 5,
        out_specs=(VMEM, VMEM),
        scratch_shapes=[pltpu.VMEM((order, order), F32)] * 3,
        cost_estimate=pl.CostEstimate(flops=15_000_000_000, bytes_accessed=4_000_000, transcendentals=0),
        name="factor_end",
    )(head_rows, below, *state)
    shared = (ids, high, low, below, fric_tiles)
    both = jax.ShapeDtypeStruct((2, rows, rows * panels // 2), F32)

    def schur(hops, own, *arrays):
        aliased = not own
        return pl.pallas_call(
            functools.partial(schur_kernel, width, panels, hops, own, aliased),
            out_shape=both,
            in_specs=[SMEM] + [VMEM] * (len(shared) - 1 + len(arrays)),
            out_specs=VMEM,
            cost_estimate=pl.CostEstimate(flops=2_000_000_000, bytes_accessed=4_000_000, transcendentals=0),
            name="schur_near" if own else "schur_far",
        )(*shared, *arrays)

    near = [x for pair in zip(ups[:-1], downs[:-1]) for x in pair]
    mixed = schur(range(1, panels - 1), True, *near)
    mixed = schur([panels - 1], False, ups[-1], downs[-1], mixed)
    partner = lax.ppermute(mixed[1], "front", [(i, i ^ 1) for i in range(groups)])
    return (mixed[0] + partner)[None]


def solution(mesh):
    return jax.shard_map(
        per_device,
        mesh=mesh,
        in_specs=(
            P("front", "panel", None, None, None),
            P("front", "panel", None, None),
            P("front", "panel", None),
            P("front", None),
        ),
        out_specs=P("front", "panel", None),
        check_vma=False,
    )
```

```python
import functools

import jax
import jax.numpy as jnp
from jax import lax
from jax.experimental import pallas as pl
from jax.experimental.pallas import tpu as pltpu
from jax.sharding import PartitionSpec as P

F32 = jnp.float32
BF16 = jnp.bfloat16
HEADER = 16
NN = (((1,), (0,)), ((), ()))
NT = (((1,), (1,)), ((), ()))
VMEM = pl.BlockSpec(memory_space=pltpu.VMEM)
SMEM = pl.BlockSpec(memory_space=pltpu.SMEM)


def split(x):
    hi = x.astype(BF16)
    return hi, (x - hi.astype(F32)).astype(BF16)


def dot(a, b, dims):
    return lax.dot_general(a, b, dims, preferred_element_type=F32)


def dot3(a, b, dims):
    ah, al = split(a)
    bh, bl = split(b)
    return dot(ah, bh, dims) + (dot(ah, bl, dims) + dot(al, bh, dims))


def pack_kernel(slots, target_ref, place_ref, tiles_ref, out_ref, count_ref, header_ref):
    tiles, edge = tiles_ref.shape[0], tiles_ref.shape[1]
    groups = out_ref.shape[0]
    header_ref[...] = jnp.zeros_like(header_ref)

    def clear(g, carry):
        count_ref[g] = 0
        return carry

    lax.fori_loop(0, groups, clear, 0)
    lane = lax.broadcasted_iota(jnp.int32, (1, edge), 1)

    def one(i, carry):
        t = target_ref[i]
        r = count_ref[t]
        count_ref[t] = r + 1
        out_ref[t, pl.ds(pl.multiple_of(r * edge, edge), edge), :] = tiles_ref[i]
        mark = (place_ref[i] + 1).astype(F32)
        header_ref[t] = jnp.where(lane == r, mark, header_ref[t])
        return carry

    lax.fori_loop(0, tiles, one, 0)

    def finish(g, carry):
        out_ref[g, pl.ds(slots * edge, HEADER), :] = jnp.broadcast_to(
            header_ref[g], (HEADER, edge)
        ).astype(BF16)
        return carry

    lax.fori_loop(0, groups, finish, 0)


def assemble_kernel(slots, panels, local_tiles, col_tiles, ids_ref, place_ref, arrived_ref, head_ref, below_ref, acc_ref):
    groups = arrived_ref.shape[0]
    edge = arrived_ref.shape[2]
    me = ids_ref[0]

    def clear(i, carry):
        acc_ref[i] = jnp.zeros((edge, edge), F32)
        return carry

    lax.fori_loop(0, local_tiles * col_tiles, clear, 0)

    def one_group(g, carry):
        def one(s, carry):
            place = place_ref[g, s]

            @pl.when(place > 0)
            def _():
                tile = arrived_ref[g, pl.ds(pl.multiple_of(s * edge, edge), edge), :]
                acc_ref[place - 1] += tile.astype(F32)

            return carry

        return lax.fori_loop(0, slots, one, carry)

    lax.fori_loop(0, groups, one_group, 0)
    row = lax.broadcasted_iota(jnp.int32, (edge, edge), 0)
    col = lax.broadcasted_iota(jnp.int32, (edge, edge), 1)
    start = 0
    for j in range(local_tiles):
        for c in range((j + 1) * panels):
            tile = acc_ref[j * col_tiles + c]
            if c >= j * panels:
                tile = jnp.where(c * edge + col < (j * panels + me) * edge + row, tile, 0.0)
            tile = tile.astype(BF16)
            if j == 0:
                head_ref[:, c * edge : (c + 1) * edge] = tile
            else:
                below_ref[:, start + c * edge : start + (c + 1) * edge] = tile
        if j > 0:
            start += (j + 1) * panels * edge


def eliminate(block):
    edge = block.shape[0]
    count = edge // 8
    sub = lax.broadcasted_iota(jnp.int32, (8, edge), 0)
    lane = lax.broadcasted_iota(jnp.int32, (8, edge), 1)
    a = [block[8 * g : 8 * g + 8] for g in range(count)]
    e = [jnp.where(lane == sub + 8 * g, 1.0, 0.0).astype(F32) for g in range(count)]
    q = []

    def across(x, k):
        return jnp.broadcast_to(x[:, k : k + 1], (8, edge))

    def down(x, k):
        return jnp.broadcast_to(x[k : k + 1], (8, edge))

    for g in range(count):
        work = [across(a[g], 8 * g + s) for s in range(8)] + [a[g], e[g]]
        for s in range(0, 8, 2):
            u, v = work[s], work[s + 1]
            p11, p21, p12, p22 = down(u, s), down(u, s + 1), down(v, s), down(v, s + 1)
            flip = 1.0 / (p11 * p22 - p12 * p21)
            p11, p21, p12, p22 = p11 * flip, p21 * flip, p12 * flip, p22 * flip
            for t in range(s + 2, 10):
                x = work[t]
                x1, x2 = down(x, s), down(x, s + 1)
                y1 = p22 * x1 - p12 * x2
                y2 = p11 * x2 - p21 * x1
                x = x - u * y1 - v * y2
                work[t] = jnp.where(sub == s, y1, jnp.where(sub == s + 1, y2, x))
        qa, qe = work[8], work[9]
        q.append(qe)
        if g + 1 < count:
            ra = [down(qa, s) for s in range(8)]
            re = [down(qe, s) for s in range(8)]
        for i in range(g + 1, count):
            xa, xe = a[i], e[i]
            cols = [across(xa, 8 * g + s) for s in range(8)]
            for s in range(8):
                xa = xa - cols[s] * ra[s]
                xe = xe - cols[s] * re[s]
            a[i], e[i] = xa, xe
    return jnp.concatenate(e, axis=0), jnp.concatenate(q, axis=0)


def stages(first, last, edge, a_ref, e_ref, q_ref):
    order = a_ref.shape[0]
    below_rows = lax.broadcasted_iota(jnp.int32, (order, 1), 0)

    def stage(b, carry):
        here = pl.ds(pl.multiple_of(b * edge, edge), edge)
        unit, ready = eliminate(a_ref[here, here])
        up = dot3(ready, a_ref[here, :], NN)
        ue = dot3(ready, e_ref[here, :], NN)
        left = dot3(a_ref[:, here], unit, NT)
        left = jnp.where(below_rows >= (b + 1) * edge, left, 0.0)
        e_ref[here, :] = dot3(unit, e_ref[here, :], NN)
        q_ref[here, :] = ue
        a_ref[...] -= dot3(left, up, NN)
        e_ref[...] -= dot3(left, ue, NN)
        return carry

    lax.fori_loop(first, last, stage, 0)


def factor_start(width, edge, last, head_ref, fric_ref, a_ref, e_ref, q_ref):
    order = head_ref.shape[0]
    head = head_ref[...]
    gram = dot(head, head, NT) * (1.0 / width)
    row = lax.broadcasted_iota(jnp.int32, (order, order), 0)
    col = lax.broadcasted_iota(jnp.int32, (order, order), 1)
    eye = row == col
    a_ref[...] = gram + jnp.where(eye, fric_ref[:, :order], 0.0)
    e_ref[...] = jnp.where(eye, 1.0, 0.0).astype(F32)
    stages(0, last, edge, a_ref, e_ref, q_ref)


def factor_end(width, edge, first, head_ref, below_ref, a_in, e_in, q_in, high_ref, low_ref, a_ref, e_ref, q_ref):
    order = head_ref.shape[0]
    a_ref[...] = a_in[...]
    e_ref[...] = e_in[...]
    q_ref[...] = q_in[...]
    stages(first, order // edge, edge, a_ref, e_ref, q_ref)
    head = head_ref[...]
    eh, el = split(e_ref[...])
    gh, gl = split(dot(eh, head, NN) + dot(el, head, NN))
    qh, ql = split(q_ref[...])
    dh, dl = split((dot(qh, head, NN) + dot(ql, head, NN)) * (1.0 / width))
    start = 0
    for j in range(high_ref.shape[0] // edge):
        mine = below_ref[:, start : start + order]
        start += (j + 2) * order
        vh, vl = split(dot(mine, gh, NT) + dot(mine, gl, NT))
        done = mine.astype(F32) - (dot(vh, dh, NN) + (dot(vh, dl, NN) + dot(vl, dh, NN)))
        th, tl = split(done)
        high_ref[j * edge : (j + 1) * edge, :] = th
        low_ref[j * edge : (j + 1) * edge, :] = tl


def trimmed(rows, panels, hops):
    return [(j + 1) * panels - hops for j in range(1, rows + 1)]


def trim_kernel(was, now, after_ref, climbing_ref, sinking_ref, up_ref, down_ref):
    edge = climbing_ref.shape[0]
    start = done = 0
    for before, after in zip(was, now):
        up_ref[:, done * edge : (done + after) * edge] = climbing_ref[:, start * edge : (start + after) * edge]
        start += before
        done += after
    down_ref[...] = sinking_ref[:, : down_ref.shape[1]]


def owner_block(width, panels, me, side, owner, own, counts, theirs_ref, high_ref, low_ref, below_ref, fric_ref, out_ref):
    edge = below_ref.shape[0]
    order = high_ref.shape[1]
    rows = high_ref.shape[0] // edge
    half = panels // 2
    starts = [0]
    for j in range(rows):
        starts.append(starts[-1] + (j + 2) * order)
    place = (owner // half + side) % 2
    base = (owner % half) * (rows * edge)
    row = lax.broadcasted_iota(jnp.int32, (edge, edge), 0)
    col = lax.broadcasted_iota(jnp.int32, (edge, edge), 1)
    first = 0
    for jc in range(rows):
        cols = pl.ds(pl.multiple_of(base + jc * edge, edge), edge)
        if jc > 0:
            out_ref[place, : jc * edge, cols] = jnp.zeros((jc * edge, edge), F32)
        if jc >= len(counts):
            out_ref[place, jc * edge :, cols] = jnp.zeros(((rows - jc) * edge, edge), F32)
            continue
        last = first + counts[jc] * edge
        span = counts[jc] * edge - order
        mine = jnp.concatenate(
            [below_ref[:, starts[j] + order : starts[j] + order + span] for j in range(jc, rows)], axis=0
        )
        total = dot(mine, theirs_ref[:, first + order : last], NT)
        total += dot(high_ref[jc * edge :, :], theirs_ref[:, first : first + order], NT)
        total += dot(low_ref[jc * edge :, :], theirs_ref[:, first : first + order], NT)
        total = total * (1.0 / width)
        first = last
        top = total[:edge]
        if own:
            top += jnp.where(row == col, fric_ref[(jc + 1) * panels + me], 0.0)
        top = jnp.where(owner * edge + col <= me * edge + row, top, 0.0)
        out_ref[place, jc * edge : (jc + 1) * edge, cols] = top
        if jc + 1 < rows:
            out_ref[place, (jc + 1) * edge :, cols] = total[edge:]


def schur_kernel(width, panels, hops, own, last_call, ids_ref, high_ref, low_ref, below_ref, fric_ref, *rest):
    rest = list(rest)
    out_ref = rest.pop()
    if last_call:
        other_ref, keep_ref, mixed_ref = rest.pop(), rest.pop(), rest.pop()
        out_ref[...] = mixed_ref[...]
    me = ids_ref[0]
    side = ids_ref[1]
    rows = high_ref.shape[0] // below_ref.shape[0]
    run = functools.partial(owner_block, width, panels, me, side)
    shared = (high_ref, low_ref, below_ref, fric_ref, out_ref)
    if own:
        run(me, True, trimmed(rows, panels, 0), below_ref, *shared)
    for hop, up_ref, down_ref in zip(hops, rest[0::2], rest[1::2]):

        @pl.when(me >= hop)
        def _():
            run(me - hop, False, trimmed(rows, panels, hop), up_ref, *shared)

        @pl.when(me + hop < panels)
        def _():
            run(me + hop, False, trimmed(rows, panels, 0)[:-1], down_ref, *shared)

    if last_call:
        keep_ref[...] = out_ref[0]
        other_ref[...] = out_ref[1]


def per_device(elem_tiles, targets, tile_places, friction):
    groups = lax.axis_size("front")
    panels = lax.axis_size("panel")
    count = elem_tiles.shape[2]
    edge = elem_tiles.shape[3]
    width = friction.shape[1]
    col_tiles = width // edge
    local_tiles = col_tiles // panels
    order = edge * panels
    slots = max(2, (2 * count + groups - 1) // groups)
    ids = jnp.stack([lax.axis_index("panel"), lax.axis_index("front") % 2]).astype(jnp.int32)

    packed = pl.pallas_call(
        functools.partial(pack_kernel, slots),
        out_shape=jax.ShapeDtypeStruct((groups, slots * edge + HEADER, edge), BF16),
        in_specs=[SMEM, SMEM, VMEM],
        out_specs=VMEM,
        scratch_shapes=[pltpu.SMEM((groups,), jnp.int32), pltpu.VMEM((groups, 1, edge), F32)],
        name="pack",
    )(targets.reshape(count), tile_places.reshape(count), elem_tiles.reshape(count, edge, edge))
    arrived = lax.all_to_all(packed, "front", split_axis=0, concat_axis=0, tiled=True)
    places = arrived[:, slots * edge, :slots].astype(jnp.int32)
    spread = sum((j + 1) * order for j in range(1, local_tiles))
    head, below = pl.pallas_call(
        functools.partial(assemble_kernel, slots, panels, local_tiles, col_tiles),
        out_shape=(
            jax.ShapeDtypeStruct((edge, order), BF16),
            jax.ShapeDtypeStruct((edge, spread), BF16),
        ),
        in_specs=[SMEM, SMEM, VMEM],
        out_specs=(VMEM, VMEM),
        scratch_shapes=[pltpu.VMEM((local_tiles * col_tiles, edge, edge), F32)],
        name="assemble",
    )(ids, places, arrived)
    head_rows = lax.all_gather(head, "panel", axis=0, tiled=True)
    rows_below = local_tiles - 1
    rows = rows_below * edge
    fric_tiles = friction.reshape(col_tiles, 1, edge)
    climb = [(i, i + 1) for i in range(panels - 1)]
    sink = [(i + 1, i) for i in range(panels - 1)]
    ups, downs = [], []
    widths = [trimmed(rows_below, panels, hop) for hop in range(panels)]

    def travel(hop, after, climbing, sinking):
        up, down = pl.pallas_call(
            functools.partial(trim_kernel, widths[hop - 1], widths[hop]),
            out_shape=(
                jax.ShapeDtypeStruct((edge, sum(widths[hop]) * edge), BF16),
                jax.ShapeDtypeStruct((edge, sum(widths[0][:-1]) * edge), BF16),
            ),
            in_specs=[pl.BlockSpec(memory_space=pl.ANY), VMEM, VMEM],
            out_specs=(VMEM, VMEM),
            name="trim",
        )(after, climbing, sinking)
        ups.append(lax.ppermute(up, "panel", climb))
        downs.append(lax.ppermute(down, "panel", sink))

    travel(1, head_rows, below, below)
    square = jax.ShapeDtypeStruct((order, order), F32)
    middle = panels // 2
    state = pl.pallas_call(
        functools.partial(factor_start, width, edge, middle),
        out_shape=(square,) * 3,
        in_specs=[VMEM, VMEM],
        out_specs=(VMEM,) * 3,
        cost_estimate=pl.CostEstimate(flops=15_000_000_000, bytes_accessed=4_000_000, transcendentals=0),
        name="factor_start",
    )(head_rows, friction)
    middle_hop = (panels + 1) // 2
    for hop in range(2, middle_hop + 1):
        travel(hop, state[0], ups[-1], downs[-1])
    high, low = pl.pallas_call(
        functools.partial(factor_end, width, edge, middle),
        out_shape=(jax.ShapeDtypeStruct((rows, order), BF16),) * 2,
        in_specs=[VMEM] * 5,
        out_specs=(VMEM, VMEM),
        scratch_shapes=[pltpu.VMEM((order, order), F32)] * 3,
        cost_estimate=pl.CostEstimate(flops=15_000_000_000, bytes_accessed=4_000_000, transcendentals=0),
        name="factor_end",
    )(head_rows, below, *state)
    for hop in range(middle_hop + 1, panels):
        travel(hop, high, ups[-1], downs[-1])
    shared = (ids, high, low, below, fric_tiles)
    both = jax.ShapeDtypeStruct((2, rows, rows * panels // 2), F32)
    half = jax.ShapeDtypeStruct(both.shape[1:], F32)

    def schur(hops, own, *arrays):
        last_call = not own
        return pl.pallas_call(
            functools.partial(schur_kernel, width, panels, hops, own, last_call),
            out_shape=(half, half) if last_call else both,
            in_specs=[SMEM] + [VMEM] * (len(shared) - 1 + len(arrays)),
            out_specs=(VMEM, VMEM) if last_call else VMEM,
            scratch_shapes=[pltpu.VMEM(both.shape, F32)] if last_call else [],
            cost_estimate=pl.CostEstimate(flops=2_000_000_000, bytes_accessed=4_000_000, transcendentals=0),
            name="schur_near" if own else "schur_far",
        )(*shared, *arrays)

    near = [x for pair in zip(ups[:-1], downs[:-1]) for x in pair]
    mixed = schur(range(1, panels - 1), True, *near)
    keep, other = schur([panels - 1], False, ups[-1], downs[-1], mixed)
    partner = lax.ppermute(other, "front", [(i, i ^ 1) for i in range(groups)])
    return (keep + partner)[None]


def solution(mesh):
    return jax.shard_map(
        per_device,
        mesh=mesh,
        in_specs=(
            P("front", "panel", None, None, None),
            P("front", "panel", None, None),
            P("front", "panel", None),
            P("front", None),
        ),
        out_specs=P("front", "panel", None),
        check_vma=False,
    )
```
